32 devices in a mesh: dp: 8 (over z, y), tensor: 4 (over x, core).
Axes of the slice: x: 2, y: 2, z: 4, core: 2. Of those that a mesh axis runs over, the one named last changes fastest.
Arguments:
- inputs: bfloat16 [8192, 1024], P(('dp', 'tensor')), may hold values from -6 to 6
- doc_ids: int32 [8, 1024], P('dp'), may hold values from 0 to 1, as said below
- w_qkv: bfloat16 [3, 1024, 1024], P(None, None, 'tensor'), may hold values from -0.1875 to 0.1875
- w_out: bfloat16 [1024, 1024], P('tensor'), may hold values from -0.1875 to 0.1875
- w_up: bfloat16 [1024, 4096], P(None, 'tensor'), may hold values from -0.1875 to 0.1875
- w_down: bfloat16 [4096, 1024], P('tensor'), may hold values from -0.09375 to 0.09375
- norm_gain: float32 [4, 1024], replicated, may hold values from 0.25 to 1.75
- norm_bias: float32 [4, 1024], replicated, may hold values from -1.5 to 1.5
- out_grad: bfloat16 [8192, 1024], P(('dp', 'tensor')), may hold values from -6 to 6
Outputs:
- output: bfloat16 [8192, 1024], P(('dp', 'tensor'))
- grad_inputs: bfloat16 [8192, 1024], P(('dp', 'tensor'))
- grad_qkv: float32 [3, 1024, 1024], P(None, None, 'tensor')
- grad_wout: float32 [1024, 1024], P('tensor')
- grad_up: float32 [1024, 4096], P(None, 'tensor')
- grad_down: float32 [4096, 1024], P('tensor')
- grad_gain: float32 [4, 1024], replicated
- grad_bias: float32 [4, 1024], replicated
The draws below stay inside these ranges and needn't reach their ends.
Inputs may be any that keep to these rules, and one draw needn't show every extreme that they name: `doc_ids`: in each group either every token is in document 0, or token i is in document i // 512; exactly half of the groups are of the first kind.
All inputs are finite; a program needn't handle non-finite values.
Results may differ from the reference program's by a relative error of at most 0.015.
Values may be sent and summed in bfloat16 or wider, within the bound.
No kernel may reach another device: no remote copies, remote signals or barrier semaphores. Data moves between devices by JAX's collectives and lax.ppermute only.
A program may use at most 128 MiB of HBM per device.

```python
import jax
import jax.numpy as jnp
from jax import lax

D = 1024
HEADS = 16
HEAD_DIM = 64
FF = 4096
GROUP = 1024
SHORT = 512
GROUPS = 8
TOKENS = 8192


def draw_doc_ids(key, part):
    order = jax.random.permutation(key, GROUPS)
    long_rows = order < GROUPS // 2
    short_ids = jnp.arange(GROUP, dtype=jnp.int32) // SHORT
    return jnp.where(long_rows[:, None], jnp.zeros((GROUPS, GROUP), jnp.int32), short_ids[None, :]).astype(jnp.int32)


def block_levels(key, extent, split, least, top_value):
    def one(dim, blocks):
        heights = jax.random.uniform(jax.random.fold_in(jax.random.fold_in(key, 6), dim), (blocks,), jnp.float32, least / len(split), top_value / len(split))
        return jnp.repeat(jnp.exp(heights), extent[dim] // blocks).reshape((-1,) + (1,) * (len(extent) - dim - 1))

    factor_of = one(*split[0])
    for cut in split[1:]:
        factor_of = factor_of * one(*cut)
    return factor_of


def normal_values(rng, shape, scale, limit, pieces=(), held_as=jnp.bfloat16):
    array = scale * jax.random.normal(rng, shape, jnp.float32)
    if pieces:
        array = array * block_levels(rng, shape, pieces, -0.22, 0.18)
    return jnp.clip(array, -limit, limit).astype(held_as)


def setup_inputs(seed: int = 0) -> dict:
    arg_keys = jax.random.split(jax.random.key(seed), 10)
    return {
        "inputs": normal_values(arg_keys[0], (TOKENS, D), 1.0, 6.0, ((0, 32),)),
        "doc_ids": draw_doc_ids(jax.random.fold_in(arg_keys[9], 71), 0),
        "w_qkv": normal_values(arg_keys[2], (3, D, D), D ** -0.5, 0.1875, ((2, 4),)),
        "w_out": normal_values(arg_keys[3], (D, D), D ** -0.5, 0.1875, ((0, 4),)),
        "w_up": normal_values(arg_keys[4], (D, FF), D ** -0.5, 0.1875, ((1, 4),)),
        "w_down": normal_values(arg_keys[5], (FF, D), FF ** -0.5, 0.09375, ((0, 4),)),
        "norm_gain": jnp.clip(1.0 + 0.15 * jax.random.normal(arg_keys[6], (4, D), jnp.float32), 0.25, 1.75),
        "norm_bias": normal_values(arg_keys[7], (4, D), 0.3, 1.5, (), jnp.float32),
        "out_grad": normal_values(arg_keys[8], (TOKENS, D), 1.0, 6.0, ((0, 32),)),
    }


eps = 1e-05

@jax.custom_vjp
def low(v):
    return lax.optimization_barrier(v.astype(jnp.bfloat16)).astype(jnp.float32)

@jax.custom_vjp
def low_back(v):
    return v

def low_keep(v):
    return (low(v), None)

def low_pass(kept, grad):
    return (grad,)

def back_keep(v):
    return (v, None)

def back_low(kept, grad):
    return (low(grad),)
low.defvjp(low_keep, low_pass)
low_back.defvjp(back_keep, back_low)

def rope_tables(doc_row):
    length_all = doc_row.shape[0]
    places = jnp.arange(length_all, dtype=jnp.int32)
    earlier = jnp.concatenate([doc_row[:1], doc_row[:-1]])
    starting = jnp.logical_and(doc_row != earlier, places > 0)
    first_pos = lax.cummax(jnp.where(starting, places, 0), axis=0)
    place = (places - first_pos).astype(jnp.float32)
    half = HEAD_DIM // 2
    freqs = 10000.0 ** (-jnp.arange(half, dtype=jnp.float32) / half)
    angles = place[:, None] * freqs[None, :]
    return (jnp.cos(angles), jnp.sin(angles))

def rotate(values_in, cosine, sine_table):
    half = values_in.shape[-1] // 2
    first = values_in[..., :half]
    second = values_in[..., half:]
    cos_wide = cosine[:, None, :]
    sin_wide = sine_table[:, None, :]
    return jnp.concatenate([first * cos_wide - second * sin_wide, second * cos_wide + first * sin_wide], axis=-1)

def block_mask(doc_row, offset, block_rows):
    places = jnp.arange(doc_row.shape[0], dtype=jnp.int32)
    query_pos = offset + jnp.arange(block_rows, dtype=jnp.int32)
    query_doc = lax.dynamic_slice_in_dim(doc_row, offset, block_rows, 0)
    return jnp.logical_and(places[None, :] <= query_pos[:, None], doc_row[None, :] == query_doc[:, None])

def layer_norm(values_in, gain, bias):
    center = values_in - lax.optimization_barrier(jnp.mean(values_in, axis=-1, keepdims=True))
    spread = lax.optimization_barrier(jnp.mean(center * center, axis=-1, keepdims=True))
    return center * lax.rsqrt(spread + eps) * gain + bias

def gelu_exact(values_in):
    return 0.5 * values_in * (1.0 + jax.scipy.special.erf(values_in * 0.7071067811865476))

def group_forward(values_in, doc_row, w_qkv, w_out, w_up, w_down, gain_rows, bias_rows):
    highest = lax.Precision.HIGHEST
    length_all = values_in.shape[0]
    cosine, sine_table = rope_tables(doc_row)
    normed = low(layer_norm(values_in, gain_rows[0], bias_rows[0]))
    shaped = (length_all, HEADS, HEAD_DIM)
    projected = [low_back(jnp.dot(normed, w_qkv[j], precision=highest)) for j in range(3)]
    query = low(rotate(projected[0].reshape(shaped), cosine, sine_table))
    key_rot = low(rotate(projected[1].reshape(shaped), cosine, sine_table))
    value_all = low(projected[2].reshape(shaped))
    block_rows = min(512, length_all)
    scaling = HEAD_DIM ** (-0.5)

    def attend(offset):
        query_block = lax.dynamic_slice_in_dim(query, offset, block_rows, 0)
        scores = low_back(jnp.einsum('qhd,khd->hqk', query_block, key_rot, precision=highest)) * scaling
        scores = jnp.where(block_mask(doc_row, offset, block_rows)[None], scores, -1e+30)
        row_max = lax.optimization_barrier(jnp.max(scores, axis=-1, keepdims=True))
        exp_scores = jnp.exp(scores - row_max)
        weights = low(exp_scores / lax.optimization_barrier(jnp.sum(exp_scores, axis=-1, keepdims=True)))
        return low(low_back(jnp.einsum('hqk,khd->qhd', weights, value_all, precision=highest)))
    offsets = jnp.arange(length_all // block_rows, dtype=jnp.int32) * block_rows
    head_out = lax.map(jax.checkpoint(attend), offsets).reshape(length_all, D)
    attended = low_back(jnp.dot(head_out, w_out, precision=highest))
    middle = values_in + layer_norm(attended, gain_rows[1], bias_rows[1])
    normed2 = low(layer_norm(middle, gain_rows[2], bias_rows[2]))
    hidden = low_back(jnp.dot(normed2, w_up, precision=highest))
    activated = low(gelu_exact(hidden))
    mixed = low_back(jnp.dot(activated, w_down, precision=highest))
    return middle + layer_norm(mixed, gain_rows[3], bias_rows[3])

def reference(inputs, doc_ids, w_qkv, w_out, w_up, w_down, norm_gain, norm_bias, out_grad):
    weights_all = (w_qkv.astype(jnp.float32), w_out.astype(jnp.float32), w_up.astype(jnp.float32), w_down.astype(jnp.float32), norm_gain.astype(jnp.float32), norm_bias.astype(jnp.float32))
    rows_in = inputs.astype(jnp.float32).reshape(GROUPS, GROUP, D)
    grads_in = out_grad.astype(jnp.float32).reshape(GROUPS, GROUP, D)

    def one_group(running, item):
        group_in, doc_row, group_grad = item

        def forward(values_in, *params):
            return group_forward(values_in, doc_row, *params)
        result, pull = jax.vjp(forward, group_in, *weights_all)
        pulled = pull(group_grad)
        running = tuple((total + extra for total, extra in zip(running, pulled[1:])))
        return (running, (result.astype(jnp.bfloat16), pulled[0].astype(jnp.bfloat16)))
    start_sums = tuple((jnp.zeros_like(param) for param in weights_all))
    sums_all, (outputs, grad_rows) = lax.scan(one_group, start_sums, (rows_in, doc_ids, grads_in))
    grad_qkv, grad_wout, grad_up, grad_down, grad_gain, grad_bias = sums_all
    return (outputs.reshape(TOKENS, D), grad_rows.reshape(TOKENS, D), grad_qkv, grad_wout, grad_up, grad_down, grad_gain, grad_bias)
```

```python
import functools

import jax
import jax.numpy as jnp
from jax import lax
from jax.experimental import pallas as pl
from jax.experimental.pallas import tpu as pltpu
from jax.sharding import PartitionSpec as P

HEAD_DIM = 64
HALF = HEAD_DIM // 2
SHORT = 512
eps = 1e-05
low = jnp.bfloat16
full = jnp.float32
NT = (((1,), (1,)), ((), ()))
TN = (((0,), (0,)), ((), ()))


def swap(values, axis, stride):
    return lax.ppermute(values, axis, [(i, i ^ stride) for i in range(lax.axis_size(axis))])


def norm_forward(values_in, gain, bias):
    center = values_in - jnp.mean(values_in, axis=-1, keepdims=True)
    spread = jnp.mean(center * center, axis=-1, keepdims=True)
    scale_inv = lax.rsqrt(spread + eps)
    unit = center * scale_inv
    return (unit * gain + bias, unit, scale_inv)


def norm_backward(upstream, unit, scale_inv, gain):
    scaled = upstream * gain
    result = scale_inv * (
        scaled
        - jnp.mean(scaled, axis=-1, keepdims=True)
        - unit * jnp.mean(scaled * unit, axis=-1, keepdims=True)
    )
    return (result, jnp.sum(upstream * unit, axis=0), jnp.sum(upstream, axis=0))


def gelu_exact(values_in):
    return 0.5 * values_in * (1.0 + lax.erf(values_in * 0.7071067811865476))


def gelu_slope(values_in):
    return (
        0.5 * (1.0 + lax.erf(values_in * 0.7071067811865476))
        + values_in * jnp.exp(-0.5 * values_in * values_in) * 0.3989422804014327
    )


def rope_tables(length_all, two_docs):
    places = jnp.arange(length_all, dtype=jnp.int32)
    place = jnp.where(jnp.logical_and(two_docs, places >= SHORT), places - SHORT, places).astype(full)
    freqs = 10000.0 ** (-jnp.arange(HALF, dtype=full) / HALF)
    angles = place[:, None] * freqs[None, :]
    cosine = jnp.cos(angles)
    sine = jnp.sin(angles)
    return (
        jnp.concatenate([cosine, cosine, cosine, cosine], axis=1),
        jnp.concatenate([-sine, sine, -sine, sine], axis=1),
    )


def turn(values, cosine, sine, back):
    lane = lax.broadcasted_iota(jnp.int32, cosine.shape, 1)
    first = (lane % HEAD_DIM) < HALF
    parts = []
    for at in range(0, values.shape[1], 128):
        part = values[:, at : at + 128]
        other = jnp.where(first, pltpu.roll(part, 128 - HALF, 1), pltpu.roll(part, HALF, 1))
        moved = other * sine
        parts.append(part * cosine - moved if back else part * cosine + moved)
    return jnp.concatenate(parts, axis=1)


def forward_kernel(meta, n0, n1, n2, n3, w, cosine, sine, q, k, v, out, logs, stage):
    rows = n0.shape[0]
    width = q.shape[1]
    heads = width // HEAD_DIM
    index = meta[0]
    barred = jnp.where(meta[1] != 0, -1e30, 0.0).astype(full)
    for j, block in enumerate((n0, n1, n2, n3)):
        at = pl.multiple_of((index ^ j) * rows, rows)
        here = pl.ds(at, rows)
        x = block[...]
        cos_part = cosine[here, :]
        sin_part = sine[here, :]
        pre = jnp.dot(x, w[0], preferred_element_type=full)
        q[here, :] = turn(pre, cos_part, sin_part, False).astype(low)
        pre = jnp.dot(x, w[1], preferred_element_type=full)
        k[here, :] = turn(pre, cos_part, sin_part, False).astype(low)
        v[here, :] = jnp.dot(x, w[2], preferred_element_type=full).astype(low)
    lane = lax.broadcasted_iota(jnp.int32, (rows, width), 1) // HEAD_DIM
    narrow = lax.broadcasted_iota(jnp.int32, (rows, 128), 1)
    low_tri = lax.broadcasted_iota(jnp.int32, (rows, rows), 0) >= lax.broadcasted_iota(
        jnp.int32, (rows, rows), 1
    )
    for block in range(4):
        begin = block * rows
        count = begin + rows
        query = q[pl.ds(begin, rows), :]

        def one(h, carry):
            acc, log_cols = carry
            mine = lane == h
            chosen = jnp.where(mine, query * jnp.asarray(HEAD_DIM**-0.5, low), jnp.zeros_like(query))
            scores = lax.dot_general(chosen, k[pl.ds(0, count), :], NT, preferred_element_type=full)
            pieces = []
            for at in range(0, count, rows):
                piece = scores[:, at : at + rows]
                if at == begin:
                    piece = jnp.where(low_tri, piece, -1e30)
                elif begin >= SHORT and at < SHORT:
                    piece = piece + barred
                pieces.append(piece)
            top = pieces[0]
            for piece in pieces[1:]:
                top = jnp.maximum(top, piece)
            top = jnp.max(top, axis=-1, keepdims=True)
            pieces = [jnp.exp(piece - top) for piece in pieces]
            total = pieces[0]
            for piece in pieces[1:]:
                total = total + piece
            total = jnp.sum(total, axis=-1, keepdims=True)
            weights = jnp.concatenate([piece.astype(low) for piece in pieces], axis=1)
            got = jnp.dot(weights, v[pl.ds(0, count), :], preferred_element_type=full)
            acc = jnp.where(mine, got / total, acc)
            log_cols = jnp.where(narrow == h, top + jnp.log(total), log_cols)
            return acc, log_cols

        acc, log_cols = lax.fori_loop(
            0,
            heads,
            one,
            (jnp.zeros((rows, width), full), jnp.zeros((rows, 128), full)),
            unroll=UNROLL,
        )
        stage[pl.ds(begin, rows), :] = acc.astype(low)
        logs[:, pl.ds(begin, rows)] = jnp.transpose(log_cols)[:8, :]
    for j in range(4):
        at = pl.multiple_of((index ^ j) * rows, rows)
        out[pl.ds(j * rows, rows), :] = stage[pl.ds(at, rows), :]


UNROLL = 2


def backward_kernel(meta, g0, g1, g2, g3, w_out, q, k, v, out, logs, cosine, sine, result, d_out, dq, dk, dv, prob, ds, delta):
    rows = g0.shape[0]
    width = q.shape[1]
    heads = width // HEAD_DIM
    index = meta[0]
    barred = jnp.where(meta[1] != 0, -1e30, 0.0).astype(full)
    picks = (
        lax.broadcasted_iota(jnp.int32, (8, width), 0)
        == lax.broadcasted_iota(jnp.int32, (8, width), 1) // HEAD_DIM
    ).astype(full)
    for j, block in enumerate((g0, g1, g2, g3)):
        at = pl.multiple_of((index ^ j) * rows, rows)
        here = pl.ds(at, rows)
        grad = lax.dot_general(block[...], w_out[...], NT, preferred_element_type=full).astype(low)
        d_out[here, :] = grad
        both = grad.astype(full) * out[pl.ds(j * rows, rows), :].astype(full)
        delta[:, here] = lax.dot_general(
            picks, both, NT, preferred_element_type=full, precision=lax.Precision.HIGHEST
        )
    lane = lax.broadcasted_iota(jnp.int32, (rows, width), 1) // HEAD_DIM
    high_tri = lax.broadcasted_iota(jnp.int32, (rows, rows), 0) <= lax.broadcasted_iota(
        jnp.int32, (rows, rows), 1
    )
    dk[...] = jnp.zeros_like(dk)
    dv[...] = jnp.zeros_like(dv)
    scale = HEAD_DIM**-0.5
    for block in range(4):
        begin = block * rows
        count = begin + rows
        here = pl.ds(begin, rows)
        query = q[here, :] * jnp.asarray(scale, low)
        grad = d_out[here, :]

        def one(h, acc):
            mine = lane == h
            chosen = jnp.where(mine, query, jnp.zeros_like(query))
            above = jnp.where(mine, grad, jnp.zeros_like(grad))
            log_row = logs[pl.ds(h, 1), here]
            delta_row = delta[pl.ds(h, 1), here]
            scores = lax.dot_general(k[pl.ds(0, count), :], chosen, NT, preferred_element_type=full)
            d_prob = lax.dot_general(v[pl.ds(0, count), :], above, NT, preferred_element_type=full)
            for at in range(0, count, rows):
                piece = scores[at : at + rows, :] - log_row
                if at == begin:
                    piece = jnp.where(high_tri, piece, -1e30)
                elif begin >= SHORT and at < SHORT:
                    piece = piece + barred
                p = jnp.exp(piece)
                prob[pl.ds(at, rows), :] = p.astype(low)
                ds[pl.ds(at, rows), :] = (p * (d_prob[at : at + rows, :] - delta_row)).astype(low)
            dv[pl.ds(0, count), :] += jnp.dot(prob[pl.ds(0, count), :], above, preferred_element_type=full)
            dk[pl.ds(0, count), :] += jnp.dot(ds[pl.ds(0, count), :], chosen, preferred_element_type=full)
            got = lax.dot_general(
                ds[pl.ds(0, count), :], k[pl.ds(0, count), :], TN, preferred_element_type=full
            )
            return jnp.where(mine, got, acc)

        acc = lax.fori_loop(0, heads, one, jnp.zeros((rows, width), full))
        dq[here, :] = acc * scale
    for j in range(4):
        at = pl.multiple_of((index ^ j) * rows, rows)
        here = pl.ds(at, rows)
        there = pl.ds(j * rows, rows)
        cos_part = cosine[here, :]
        sin_part = sine[here, :]
        result[0, there, :] = turn(dq[here, :], cos_part, sin_part, True).astype(low)
        result[1, there, :] = turn(dk[here, :], cos_part, sin_part, True).astype(low)
        result[2, there, :] = dv[here, :].astype(low)


def in_vmem(count):
    return [pl.BlockSpec(memory_space=pltpu.SMEM)] + [
        pl.BlockSpec(memory_space=pltpu.VMEM) for _ in range(count)
    ]


def attention_forward(meta, blocks, w_qkv, cosine, sine):
    length = cosine.shape[0]
    width = w_qkv.shape[2]
    shaped = jax.ShapeDtypeStruct((length, width), low)
    return pl.pallas_call(
        forward_kernel,
        out_shape=(shaped, shaped, shaped, shaped, jax.ShapeDtypeStruct((8, length), full)),
        in_specs=in_vmem(7),
        out_specs=tuple(pl.BlockSpec(memory_space=pltpu.VMEM) for _ in range(5)),
        scratch_shapes=[pltpu.VMEM((length, width), low)],
        name="attend",
    )(meta, *blocks, w_qkv, cosine, sine)


def attention_backward(meta, blocks, w_out, q, k, v, out, logs, cosine, sine):
    length = cosine.shape[0]
    width = q.shape[1]
    rows = blocks[0].shape[0]
    return pl.pallas_call(
        backward_kernel,
        out_shape=jax.ShapeDtypeStruct((3, length, width), low),
        in_specs=in_vmem(12),
        out_specs=pl.BlockSpec(memory_space=pltpu.VMEM),
        scratch_shapes=[
            pltpu.VMEM((length, width), low),
            pltpu.VMEM((length, width), full),
            pltpu.VMEM((length, width), full),
            pltpu.VMEM((length, width), full),
            pltpu.VMEM((length, rows), low),
            pltpu.VMEM((length, rows), low),
            pltpu.VMEM((8, length), full),
        ],
        name="attend_back",
    )(meta, *blocks, w_out, q, k, v, out, logs, cosine, sine)


def assemble_kernel(parts, meta, mine, other, result):
    size = mine.shape[0]
    owner = meta[0]
    step = 2 * size // parts
    for i in range(parts):
        source = mine if i < parts // 2 else other
        begin = (i % (parts // 2)) * step
        at = pl.multiple_of((owner ^ i) * step, step)
        result[pl.ds(at, step), :] = source[pl.ds(begin, step), :].astype(full)


def assemble(meta, mine, other, parts):
    rows, width = mine.shape
    return pl.pallas_call(
        functools.partial(assemble_kernel, parts),
        out_shape=jax.ShapeDtypeStruct((2 * rows, width), full),
        in_specs=in_vmem(2),
        out_specs=pl.BlockSpec(memory_space=pltpu.VMEM),
        name="assemble",
    )(meta, mine, other)


CUTS = 3


def dp_sum(partial):
    size = lax.axis_size("dp")
    index = lax.axis_index("dp")
    bits = size.bit_length() - 1
    cuts = min(CUTS, bits)
    current = partial
    owner = jnp.int32(0)
    for b in range(cuts):
        bit = (index >> b) & 1
        owner = owner * 2 + bit
        half = current.shape[0] // 2
        sent = lax.dynamic_slice_in_dim(current, (1 - bit) * half, half, 0)
        kept = lax.dynamic_slice_in_dim(current, bit * half, half, 0)
        came = swap(sent, "dp", 1 << b)
        current = (kept.astype(full) + came.astype(full)).astype(low)
    for b in range(cuts, bits):
        current = (current.astype(full) + swap(current, "dp", 1 << b).astype(full)).astype(low)
    for b in reversed(range(1, cuts)):
        current = jnp.concatenate([current, swap(current, "dp", 1 << b)], axis=0)
    other = swap(current, "dp", 1)
    meta = jnp.stack([owner, owner])
    return assemble(meta, current, other, 1 << cuts)


def gather(values):
    near = swap(values, "tensor", 1)
    far = swap(values, "tensor", 2)
    last = swap(far, "tensor", 1)
    return values, near, far, last


def reduce_rows(far_part, near_part):
    own = far_part.shape[0] // 2
    came = swap(far_part[own:].astype(low), "tensor", 1)
    crossing = swap((far_part[:own] + came.astype(full)).astype(low), "tensor", 2)
    beside = swap(near_part[own:].astype(low), "tensor", 1)
    return near_part[:own] + beside.astype(full) + crossing.astype(full)


def mm(a, b):
    return jnp.dot(a, b, preferred_element_type=full)


def per_device(inputs, doc_ids, w_qkv, w_out, w_up, w_down, norm_gain, norm_bias, out_grad):
    doc_row = doc_ids[0]
    length_all = doc_row.shape[0]
    two_docs = doc_row[length_all - 1] != doc_row[0]
    index = lax.axis_index("tensor").astype(jnp.int32)
    meta = jnp.stack([index, two_docs.astype(jnp.int32)])
    cosine, sine = rope_tables(length_all, two_docs)
    rows_f32 = inputs.astype(full)
    normed, unit0, inv0 = norm_forward(rows_f32, norm_gain[0], norm_bias[0])
    blocks0 = gather(normed.astype(low))
    q, k, v, head_out, logs = attention_forward(meta, blocks0, w_qkv, cosine, sine)
    side = length_all // 2
    attended = reduce_rows(mm(head_out[side:], w_out), mm(head_out[:side], w_out))
    attn_normed, unit1, inv1 = norm_forward(attended, norm_gain[1], norm_bias[1])
    middle = rows_f32 + attn_normed
    normed2, unit2, inv2 = norm_forward(middle, norm_gain[2], norm_bias[2])
    blocks2 = gather(normed2.astype(low))
    near2 = jnp.concatenate(blocks2[:2], axis=0)
    far2 = jnp.concatenate(blocks2[2:], axis=0)
    hidden_near = mm(near2, w_up)
    active_near = gelu_exact(hidden_near).astype(low)
    mixed_near = mm(active_near, w_down)
    hidden_far = mm(far2, w_up)
    active_far = gelu_exact(hidden_far).astype(low)
    mixed = reduce_rows(mm(active_far, w_down), mixed_near)
    mixed_normed, unit3, inv3 = norm_forward(mixed, norm_gain[3], norm_bias[3])
    output = (middle + mixed_normed).astype(low)
    grad_out = out_grad.astype(full)
    grad_mixed, gain3, bias3 = norm_backward(grad_out, unit3, inv3, norm_gain[3])
    blocks3 = gather(grad_mixed.astype(low))
    near3 = jnp.concatenate(blocks3[:2], axis=0)
    far3 = jnp.concatenate(blocks3[2:], axis=0)

    def back_up(grad_all, hidden):
        grad_act = lax.dot_general(grad_all, w_down, NT, preferred_element_type=full)
        return (grad_act * gelu_slope(hidden)).astype(low)

    grad_hidden_near = back_up(near3, hidden_near)
    term_near = lax.dot_general(grad_hidden_near, w_up, NT, preferred_element_type=full)
    grad_hidden_far = back_up(far3, hidden_far)
    term_far = lax.dot_general(grad_hidden_far, w_up, NT, preferred_element_type=full)
    grad_normed2 = reduce_rows(term_far, term_near)
    active = jnp.concatenate([active_near, active_far], axis=0)
    grad_mixed_all = jnp.concatenate([near3, far3], axis=0)
    part_down = lax.dot_general(active, grad_mixed_all, TN, preferred_element_type=full).astype(low)
    grad_down = dp_sum(part_down)
    normed2_all = jnp.concatenate([near2, far2], axis=0)
    grad_hidden = jnp.concatenate([grad_hidden_near, grad_hidden_far], axis=0)
    part_up = lax.dot_general(normed2_all, grad_hidden, TN, preferred_element_type=full).astype(low)
    grad_up = dp_sum(part_up)
    back2, gain2, bias2 = norm_backward(grad_normed2, unit2, inv2, norm_gain[2])
    grad_middle = grad_out + back2
    grad_attended, gain1, bias1 = norm_backward(grad_middle, unit1, inv1, norm_gain[1])
    blocks1 = gather(grad_attended.astype(low))
    grad_proj = attention_backward(meta, blocks1, w_out, q, k, v, head_out, logs, cosine, sine)
    grad_attended_all = jnp.concatenate(blocks1, axis=0)
    part_wout = lax.dot_general(head_out, grad_attended_all, TN, preferred_element_type=full).astype(low)
    grad_wout = dp_sum(part_wout)

    def qkv_term(part):
        total = 0.0
        for j in range(3):
            total = total + lax.dot_general(part[j], w_qkv[j], NT, preferred_element_type=full)
        return total

    grad_normed = reduce_rows(qkv_term(grad_proj[:, side:]), qkv_term(grad_proj[:, :side]))
    normed_all = jnp.concatenate(blocks0, axis=0)
    part_qkv = jnp.concatenate(
        [
            lax.dot_general(normed_all, grad_proj[j], TN, preferred_element_type=full).astype(low)
            for j in range(3)
        ],
        axis=0,
    )
    grad_qkv = dp_sum(part_qkv).reshape(w_qkv.shape)
    back0, gain0, bias0 = norm_backward(grad_normed, unit0, inv0, norm_gain[0])
    grad_inputs = (grad_middle + back0).astype(low)
    small = jnp.stack([gain0, gain1, gain2, gain3, bias0, bias1, bias2, bias3], axis=0)
    for axis in ("tensor", "dp"):
        stride = 1
        while stride < lax.axis_size(axis):
            small = small + swap(small, axis, stride)
            stride *= 2
    return (output, grad_inputs, grad_qkv, grad_wout, grad_up, grad_down, small[:4], small[4:])


def solution(mesh):
    return jax.shard_map(
        per_device,
        mesh=mesh,
        in_specs=(
            P(("dp", "tensor"), None),
            P("dp", None),
            P(None, None, "tensor"),
            P("tensor", None),
            P(None, "tensor"),
            P("tensor", None),
            P(),
            P(),
            P(("dp", "tensor"), None),
        ),
        out_specs=(
            P(("dp", "tensor"), None),
            P(("dp", "tensor"), None),
            P(None, None, "tensor"),
            P("tensor", None),
            P(None, "tensor"),
            P("tensor", None),
            P(),
            P(),
        ),
        check_vma=False,
    )
```

```python
import functools

import jax
import jax.numpy as jnp
from jax import lax
from jax.experimental import pallas as pl
from jax.experimental.pallas import tpu as pltpu
from jax.sharding import PartitionSpec as P

HEAD_DIM = 64
HALF = HEAD_DIM // 2
SHORT = 512
eps = 1e-05
low = jnp.bfloat16
full = jnp.float32
NT = (((1,), (1,)), ((), ()))
TN = (((0,), (0,)), ((), ()))


def swap(values, axis, stride):
    return lax.ppermute(values, axis, [(i, i ^ stride) for i in range(lax.axis_size(axis))])


def norm_forward(values_in, gain, bias):
    center = values_in - jnp.mean(values_in, axis=-1, keepdims=True)
    spread = jnp.mean(center * center, axis=-1, keepdims=True)
    scale_inv = lax.rsqrt(spread + eps)
    unit = center * scale_inv
    return (unit * gain + bias, unit, scale_inv)


def norm_backward(upstream, unit, scale_inv, gain):
    scaled = upstream * gain
    result = scale_inv * (
        scaled
        - jnp.mean(scaled, axis=-1, keepdims=True)
        - unit * jnp.mean(scaled * unit, axis=-1, keepdims=True)
    )
    return (result, jnp.sum(upstream * unit, axis=0), jnp.sum(upstream, axis=0))


def gelu_exact(values_in):
    return 0.5 * values_in * (1.0 + lax.erf(values_in * 0.7071067811865476))


def gelu_slope(values_in):
    return (
        0.5 * (1.0 + lax.erf(values_in * 0.7071067811865476))
        + values_in * jnp.exp(-0.5 * values_in * values_in) * 0.3989422804014327
    )


def rope_tables(length_all, two_docs):
    places = jnp.arange(length_all, dtype=jnp.int32)
    place = jnp.where(jnp.logical_and(two_docs, places >= SHORT), places - SHORT, places).astype(full)
    freqs = 10000.0 ** (-jnp.arange(HALF, dtype=full) / HALF)
    angles = place[:, None] * freqs[None, :]
    cosine = jnp.cos(angles)
    sine = jnp.sin(angles)
    return (
        jnp.concatenate([cosine, cosine, cosine, cosine], axis=1),
        jnp.concatenate([-sine, sine, -sine, sine], axis=1),
    )


def turn(values, cosine, sine, back):
    lane = lax.broadcasted_iota(jnp.int32, cosine.shape, 1)
    first = (lane % HEAD_DIM) < HALF
    parts = []
    for at in range(0, values.shape[1], 128):
        part = values[:, at : at + 128]
        other = jnp.where(first, pltpu.roll(part, 128 - HALF, 1), pltpu.roll(part, HALF, 1))
        moved = other * sine
        parts.append(part * cosine - moved if back else part * cosine + moved)
    return jnp.concatenate(parts, axis=1)


def forward_kernel(meta, n0, n1, n2, n3, w, cosine, sine, q, k, v, out_near, out_far, logs, stage):
    rows = n0.shape[0]
    width = q.shape[1]
    heads = width // HEAD_DIM
    index = meta[0]
    barred = jnp.where(meta[1] != 0, -1e30, 0.0).astype(full)
    for j, block in enumerate((n0, n1, n2, n3)):
        at = pl.multiple_of((index ^ j) * rows, rows)
        here = pl.ds(at, rows)
        x = block[...]
        cos_part = cosine[here, :]
        sin_part = sine[here, :]
        pre = jnp.dot(x, w[0], preferred_element_type=full)
        q[here, :] = turn(pre, cos_part, sin_part, False).astype(low)
        pre = jnp.dot(x, w[1], preferred_element_type=full)
        k[here, :] = turn(pre, cos_part, sin_part, False).astype(low)
        v[here, :] = jnp.dot(x, w[2], preferred_element_type=full).astype(low)
    lane = lax.broadcasted_iota(jnp.int32, (rows, width), 1) // HEAD_DIM
    narrow = lax.broadcasted_iota(jnp.int32, (rows, 128), 1)
    low_tri = lax.broadcasted_iota(jnp.int32, (rows, rows), 0) >= lax.broadcasted_iota(
        jnp.int32, (rows, rows), 1
    )
    for block in range(4):
        begin = block * rows
        count = begin + rows
        query = q[pl.ds(begin, rows), :]
        acc = jnp.zeros((rows, width), full)
        log_cols = jnp.zeros((rows, 128), full)
        for h in range(heads):
            mine = lane == h
            chosen = jnp.where(mine, query * jnp.asarray(HEAD_DIM**-0.5, low), jnp.zeros_like(query))
            scores = lax.dot_general(chosen, k[pl.ds(0, count), :], NT, preferred_element_type=full)
            pieces = []
            for at in range(0, count, rows):
                piece = scores[:, at : at + rows]
                if at == begin:
                    piece = jnp.where(low_tri, piece, -1e30)
                elif begin >= SHORT and at < SHORT:
                    piece = piece + barred
                pieces.append(piece)
            top = pieces[0]
            for piece in pieces[1:]:
                top = jnp.maximum(top, piece)
            top = jnp.max(top, axis=-1, keepdims=True)
            pieces = [jnp.exp(piece - top) for piece in pieces]
            total = pieces[0]
            for piece in pieces[1:]:
                total = total + piece
            total = jnp.sum(total, axis=-1, keepdims=True)
            weights = jnp.concatenate([piece.astype(low) for piece in pieces], axis=1)
            got = jnp.dot(weights, v[pl.ds(0, count), :], preferred_element_type=full)
            acc = jnp.where(mine, got / total, acc)
            log_cols = jnp.where(narrow == h, top + jnp.log(total), log_cols)
        stage[pl.ds(begin, rows), :] = acc.astype(low)
        logs[:, pl.ds(begin, rows)] = jnp.transpose(log_cols)[:8, :]
    for j in range(4):
        at = pl.multiple_of((index ^ j) * rows, rows)
        target = out_near if j < 2 else out_far
        target[pl.ds((j % 2) * rows, rows), :] = stage[pl.ds(at, rows), :]


def backward_kernel(pair, *refs):
    meta, g0, g1, g2, g3, w_out, q, k, v, out_near, out_far, logs, cosine, sine = refs[:14]
    if pair:
        before, w_qkv, result, far_term, near_term = refs[14:19]
        scratch = refs[19:]
    else:
        result = refs[14]
        scratch = refs[15:]
    d_out, dq, dk, dv, prob, ds, delta = scratch
    rows = g0.shape[0]
    width = q.shape[1]
    index = meta[0]
    barred = jnp.where(meta[1] != 0, -1e30, 0.0).astype(full)
    picks = (
        lax.broadcasted_iota(jnp.int32, (8, width), 0)
        == lax.broadcasted_iota(jnp.int32, (8, width), 1) // HEAD_DIM
    ).astype(full)
    for j, block in enumerate((g0, g1, g2, g3)):
        at = pl.multiple_of((index ^ j) * rows, rows)
        here = pl.ds(at, rows)
        grad = lax.dot_general(block[...], w_out[...], NT, preferred_element_type=full).astype(low)
        d_out[here, :] = grad
        out = out_near if j < 2 else out_far
        both = grad.astype(full) * out[pl.ds((j % 2) * rows, rows), :].astype(full)
        delta[:, here] = lax.dot_general(
            picks, both, NT, preferred_element_type=full, precision=lax.Precision.HIGHEST
        )
    lane = lax.broadcasted_iota(jnp.int32, (rows, width), 1) // HEAD_DIM
    high_tri = lax.broadcasted_iota(jnp.int32, (rows, rows), 0) <= lax.broadcasted_iota(
        jnp.int32, (rows, rows), 1
    )
    dk[...] = jnp.zeros_like(dk)
    dv[...] = jnp.zeros_like(dv)
    scale = HEAD_DIM**-0.5
    heads = width // HEAD_DIM
    for block in range(4):
        begin = block * rows
        count = begin + rows
        here = pl.ds(begin, rows)
        query = q[here, :] * jnp.asarray(scale, low)
        grad = d_out[here, :]
        acc = jnp.zeros((rows, width), full)
        for h in range(heads):
            mine = lane == h
            chosen = jnp.where(mine, query, jnp.zeros_like(query))
            above = jnp.where(mine, grad, jnp.zeros_like(grad))
            log_row = logs[pl.ds(pair * heads + h, 1), here]
            delta_row = delta[pl.ds(h, 1), here]
            scores = lax.dot_general(k[pl.ds(0, count), :], chosen, NT, preferred_element_type=full)
            d_prob = lax.dot_general(v[pl.ds(0, count), :], above, NT, preferred_element_type=full)
            for at in range(0, count, rows):
                piece = scores[at : at + rows, :] - log_row
                if at == begin:
                    piece = jnp.where(high_tri, piece, -1e30)
                elif begin >= SHORT and at < SHORT:
                    piece = piece + barred
                p = jnp.exp(piece)
                prob[h, pl.ds(at, rows), :] = p.astype(low)
                ds[h, pl.ds(at, rows), :] = (p * (d_prob[at : at + rows, :] - delta_row)).astype(low)
            dv[pl.ds(0, count), :] += jnp.dot(
                prob[h, pl.ds(0, count), :], above, preferred_element_type=full
            )
            dk[pl.ds(0, count), :] += jnp.dot(
                ds[h, pl.ds(0, count), :], chosen, preferred_element_type=full
            )
            got = lax.dot_general(
                ds[h, pl.ds(0, count), :], k[pl.ds(0, count), :], TN, preferred_element_type=full
            )
            acc = jnp.where(mine, got, acc)
        dq[here, :] = acc * scale
    for j in (2, 3, 0, 1):
        at = pl.multiple_of((index ^ j) * rows, rows)
        here = pl.ds(at, rows)
        there = pl.ds(j * rows, rows)
        cos_part = cosine[here, :]
        sin_part = sine[here, :]
        parts = (
            turn(dq[here, :], cos_part, sin_part, True).astype(low),
            turn(dk[here, :], cos_part, sin_part, True).astype(low),
            dv[here, :].astype(low),
        )
        for n, part in enumerate(parts):
            result[there, n * width : (n + 1) * width] = part
        if pair:
            total = jnp.zeros((rows, w_qkv.shape[1]), full)
            for n, part in enumerate(parts):
                wide = jnp.concatenate([before[there, n * width : (n + 1) * width], part], axis=1)
                total = total + lax.dot_general(wide, w_qkv[n], NT, preferred_element_type=full)
            target = near_term if j < 2 else far_term
            target[pl.ds((j % 2) * rows, rows), :] = total


def in_vmem(count):
    return [pl.BlockSpec(memory_space=pltpu.SMEM)] + [
        pl.BlockSpec(memory_space=pltpu.VMEM) for _ in range(count)
    ]


def attention_forward(meta, blocks, w_qkv, cosine, sine):
    length = cosine.shape[0]
    width = w_qkv.shape[2]
    shaped = jax.ShapeDtypeStruct((length, width), low)
    halved = jax.ShapeDtypeStruct((length // 2, width), low)
    return pl.pallas_call(
        forward_kernel,
        out_shape=(shaped, shaped, shaped, halved, halved, jax.ShapeDtypeStruct((8, length), full)),
        in_specs=in_vmem(7),
        out_specs=tuple(pl.BlockSpec(memory_space=pltpu.VMEM) for _ in range(6)),
        scratch_shapes=[pltpu.VMEM((length, width), low)],
        cost_estimate=pl.CostEstimate(flops=8_000_000_000, transcendentals=3_000_000, bytes_accessed=8_000_000),
        name="attend",
    )(meta, *blocks, w_qkv, cosine, sine)


def attention_backward(pair, meta, blocks, w_out, q, k, v, outs, logs, cosine, sine, before=None, w_qkv=None):
    length = cosine.shape[0]
    width = 128
    rows = blocks[0].shape[0]
    wide = blocks[0].shape[1]

    def whole(a):
        return pl.BlockSpec(a.shape, lambda i: (0,) * a.ndim)

    def columns(a):
        return pl.BlockSpec((a.shape[0], width), lambda i: (0, pair))

    args = [*blocks, w_out, q, k, v, *outs, logs, cosine, sine]
    specs = [whole(b) for b in blocks]
    specs += [pl.BlockSpec((width, wide), lambda i: (pair, 0))]
    specs += [columns(a) for a in (q, k, v, *outs)]
    specs += [whole(a) for a in (logs, cosine, sine)]
    shapes = [jax.ShapeDtypeStruct((length, 3 * width), low)]
    if pair:
        args += [before, w_qkv]
        specs += [whole(before), whole(w_qkv)]
        shapes += [jax.ShapeDtypeStruct((length // 2, wide), full)] * 2
    return pl.pallas_call(
        functools.partial(backward_kernel, pair),
        grid=(1,),
        out_shape=tuple(shapes),
        in_specs=[pl.BlockSpec(memory_space=pltpu.SMEM)] + specs,
        out_specs=tuple(pl.BlockSpec(a.shape, lambda i: (0, 0)) for a in shapes),
        scratch_shapes=[
            pltpu.VMEM((length, width), low),
            pltpu.VMEM((length, width), full),
            pltpu.VMEM((length, width), full),
            pltpu.VMEM((length, width), full),
            pltpu.VMEM((2, length, rows), low),
            pltpu.VMEM((2, length, rows), low),
            pltpu.VMEM((8, length), full),
        ],
        cost_estimate=pl.CostEstimate(flops=8_000_000_000, transcendentals=1_500_000, bytes_accessed=8_000_000),
        name=f"attend_back{pair}",
    )(meta, *args)


def place_blocks(parts, owner, mine, other, target):
    size = mine.shape[0]
    step = 2 * size // parts
    for i in range(parts):
        source = mine if i < parts // 2 else other
        begin = (i % (parts // 2)) * step
        at = pl.multiple_of((owner ^ i) * step, step)
        target[pl.ds(at, step), :] = source[pl.ds(begin, step), :].astype(target.dtype)


def assemble_kernel(parts, meta, mine, other, result):
    place_blocks(parts, meta[0], mine, other, result)


def assemble(owner, mine, other, parts):
    rows, width = mine.shape
    return pl.pallas_call(
        functools.partial(assemble_kernel, parts),
        out_shape=jax.ShapeDtypeStruct((2 * rows, width), full),
        in_specs=in_vmem(2),
        out_specs=pl.BlockSpec(memory_space=pltpu.VMEM),
        cost_estimate=pl.CostEstimate(flops=0, transcendentals=0, bytes_accessed=8_000_000),
        name="assemble",
    )(owner[None], mine, other)


def spread_kernel(parts, meta, mine0, other0, mine1, other1, qkv, wout, stage):
    width = 128
    for pair, (mine, other) in enumerate(((mine0, other0), (mine1, other1))):
        place_blocks(parts, meta[0], mine, other, stage)
        here = slice(pair * width, (pair + 1) * width)
        for n in range(3):
            qkv[n, :, here] = jnp.transpose(stage[n * width : (n + 1) * width, :].astype(full))
        wout[here, :] = stage[3 * width :, :].astype(full)


def spread(owner, first, second, parts):
    rows, wide = first[0].shape
    return pl.pallas_call(
        functools.partial(spread_kernel, parts),
        out_shape=(
            jax.ShapeDtypeStruct((3, wide, rows), full),
            jax.ShapeDtypeStruct((rows, wide), full),
        ),
        in_specs=in_vmem(4),
        out_specs=tuple(pl.BlockSpec(memory_space=pltpu.VMEM) for _ in range(2)),
        scratch_shapes=[pltpu.VMEM((2 * rows, wide), low)],
        cost_estimate=pl.CostEstimate(flops=0, transcendentals=0, bytes_accessed=8_000_000),
        name="spread",
    )(owner[None], *first, *second)


def norm0_kernel(x, gain, bias, result):
    values = x[...].astype(full)
    normed, _, _ = norm_forward(values, gain[0:1, :], bias[0:1, :])
    result[...] = normed.astype(low)


def norm0(x, gain, bias):
    return pl.pallas_call(
        norm0_kernel,
        out_shape=jax.ShapeDtypeStruct(x.shape, low),
        in_specs=[pl.BlockSpec(memory_space=pltpu.VMEM)] * 3,
        out_specs=pl.BlockSpec(memory_space=pltpu.VMEM),
        name="norm0",
    )(x, gain, bias)


def tie(*values):
    return lax.optimization_barrier(values)


CUTS = 3


class Flow:
    def __init__(self, partial, anchor):
        self.index = lax.axis_index("dp")
        self.bits = lax.axis_size("dp").bit_length() - 1
        self.cuts = min(CUTS, self.bits)
        self.plan = [("halve", b) for b in range(self.cuts)]
        self.plan += [("add", b) for b in range(self.cuts, self.bits)]
        self.plan += [("double", b) for b in reversed(range(self.cuts))]
        self.owner = jnp.int32(0)
        for b in range(self.cuts):
            self.owner = self.owner * 2 + ((self.index >> b) & 1)
        self.current = partial
        self.anchor = anchor
        self.launch()

    def launch(self):
        kind, b = self.plan[0]
        if kind == "halve":
            bit = (self.index >> b) & 1
            half = self.current.shape[0] // 2
            sent = lax.dynamic_slice_in_dim(self.current, (1 - bit) * half, half, 0)
            kept = lax.dynamic_slice_in_dim(self.current, bit * half, half, 0)
            self.kept = kept
        else:
            sent = self.current
            self.kept = self.current
        sent, self.anchor = tie(sent, self.anchor)
        self.came = swap(sent, "dp", 1 << b)

    def advance(self, anchor):
        came, anchor = tie(self.came, anchor)
        kind, _ = self.plan.pop(0)
        self.anchor = anchor
        if kind == "double":
            if not self.plan:
                self.pieces = (self.kept, came)
                return self.anchor
            self.current = jnp.concatenate([self.kept, came], axis=0)
        else:
            self.current = (self.kept.astype(full) + came.astype(full)).astype(low)
        self.launch()
        return self.anchor


def gather_start(values):
    return values, swap(values, "tensor", 1), swap(values, "tensor", 2)


def mm(a, b):
    return jnp.dot(a, b, preferred_element_type=full)


def mm_nt(a, b):
    return lax.dot_general(a, b, NT, preferred_element_type=full)


def mm_tn(a, b):
    return lax.dot_general(a, b, TN, preferred_element_type=full).astype(low)


def cross(far_part):
    own = far_part.shape[0] // 2
    came = swap(far_part[own:].astype(low), "tensor", 1)
    return (far_part[:own] + came.astype(full)).astype(low)


def beside(near_part):
    own = near_part.shape[0] // 2
    return near_part[:own] + swap(near_part[own:].astype(low), "tensor", 1).astype(full)


def per_device(inputs, doc_ids, w_qkv, w_out, w_up, w_down, norm_gain, norm_bias, out_grad):
    doc_row = doc_ids[0]
    length_all = doc_row.shape[0]
    own0, next0, across0 = gather_start(norm0(inputs, norm_gain, norm_bias))
    two_docs = doc_row[length_all - 1] != doc_row[0]
    index = lax.axis_index("tensor").astype(jnp.int32)
    meta = jnp.stack([index, two_docs.astype(jnp.int32)])
    cosine, sine = rope_tables(length_all, two_docs)
    rows_f32 = inputs.astype(full)
    across0, cosine, sine = tie(across0, cosine, sine)
    blocks0 = (own0, next0, across0, swap(across0, "tensor", 1))
    q, k, v, out_near, out_far, logs = attention_forward(meta, blocks0, w_qkv, cosine, sine)
    sent = cross(mm(out_far, w_out))
    sent, near_in = tie(sent, out_near)
    came = swap(sent, "tensor", 2)
    attended = beside(mm(near_in, w_out))
    _, unit0, inv0 = norm_forward(rows_f32, norm_gain[0], norm_bias[0])
    came, attended = tie(came, attended)
    attended = attended + came.astype(full)
    attn_normed, unit1, inv1 = norm_forward(attended, norm_gain[1], norm_bias[1])
    middle = rows_f32 + attn_normed
    normed2, unit2, inv2 = norm_forward(middle, norm_gain[2], norm_bias[2])
    own2, next2, across2 = gather_start(normed2.astype(low))
    near2 = jnp.concatenate([own2, next2], axis=0)
    hidden_near = mm(near2, w_up)
    active_near = gelu_exact(hidden_near).astype(low)
    mixed = beside(mm(active_near, w_down))
    across2, mixed = tie(across2, mixed)
    far2 = jnp.concatenate([across2, swap(across2, "tensor", 1)], axis=0)
    hidden_far = mm(far2, w_up)
    active_far = gelu_exact(hidden_far).astype(low)
    sent = cross(mm(active_far, w_down))
    sent, near2, far2, active_near, active_far = tie(sent, near2, far2, active_near, active_far)
    came = swap(sent, "tensor", 2)
    active = jnp.concatenate([active_near, active_far], axis=0)
    normed2_all = jnp.concatenate([near2, far2], axis=0)
    normed_all = jnp.concatenate(blocks0, axis=0)
    came, active, normed2_all, normed_all = tie(came, active, normed2_all, normed_all)
    mixed = mixed + came.astype(full)
    mixed_normed, unit3, inv3 = norm_forward(mixed, norm_gain[3], norm_bias[3])
    grad_out = out_grad.astype(full)
    grad_mixed, gain3, bias3 = norm_backward(grad_out, unit3, inv3, norm_gain[3])
    own3, next3, across3 = gather_start(grad_mixed.astype(low))
    output = (middle + mixed_normed).astype(low)
    near3 = jnp.concatenate([own3, next3], axis=0)
    grad_hidden_near = (mm_nt(near3, w_down) * gelu_slope(hidden_near)).astype(low)
    grad_normed2 = beside(mm_nt(grad_hidden_near, w_up))
    across3, grad_normed2, output = tie(across3, grad_normed2, output)
    far3 = jnp.concatenate([across3, swap(across3, "tensor", 1)], axis=0)
    grad_hidden_far = (mm_nt(far3, w_down) * gelu_slope(hidden_far)).astype(low)
    sent = cross(mm_nt(grad_hidden_far, w_up))
    sent, near3, far3 = tie(sent, near3, far3)
    came = swap(sent, "tensor", 2)
    grad_mixed_all = jnp.concatenate([near3, far3], axis=0)
    grad_hidden = jnp.concatenate([grad_hidden_near, grad_hidden_far], axis=0)
    down = Flow(mm_tn(active, grad_mixed_all), normed2_all)
    up = Flow(mm_tn(down.anchor, grad_hidden), grad_normed2)
    came, grad_normed2 = tie(came, up.anchor)
    grad_normed2 = grad_normed2 + came.astype(full)
    back2, gain2, bias2 = norm_backward(grad_normed2, unit2, inv2, norm_gain[2])
    grad_middle = grad_out + back2
    grad_attended, gain1, bias1 = norm_backward(grad_middle, unit1, inv1, norm_gain[1])
    own1, next1, across1 = gather_start(grad_attended.astype(low))
    next1 = down.advance(next1)
    across1, next1 = tie(across1, next1)
    blocks1 = (own1, next1, across1, swap(across1, "tensor", 1))
    outs = (out_near, out_far)
    (proj0,) = attention_backward(0, meta, blocks1, w_out, q, k, v, outs, logs, cosine, sine)
    proj0 = down.advance(proj0)
    grad_attended_all = jnp.concatenate(blocks1, axis=0)
    out_all = jnp.concatenate(outs, axis=0)

    def projections(pair, proj):
        here = slice(pair * 128, (pair + 1) * 128)
        return jnp.concatenate(
            [mm_tn(proj, normed_all), mm_tn(out_all[:, here], grad_attended_all)], axis=0
        )

    first = Flow(projections(0, proj0), proj0)
    proj1, far_term, near_term = attention_backward(
        1, meta, blocks1, w_out, q, k, v, outs, logs, cosine, sine, first.anchor, w_qkv
    )
    sent = cross(far_term)
    sent, near_term, proj1 = tie(sent, near_term, proj1)
    came = swap(sent, "tensor", 2)
    proj1 = up.advance(proj1)
    proj1 = down.advance(proj1)
    second = Flow(projections(1, proj1), proj1)
    near_term, _ = tie(near_term, second.anchor)
    grad_normed = beside(near_term)
    grad_normed = first.advance(grad_normed)
    came, grad_normed = tie(came, grad_normed)
    grad_normed = grad_normed + came.astype(full)
    back0, gain0, bias0 = norm_backward(grad_normed, unit0, inv0, norm_gain[0])
    grad_inputs = (grad_middle + back0).astype(low)
    small = jnp.stack([gain0, gain1, gain2, gain3, bias0, bias1, bias2, bias3], axis=0)
    steps = []
    for axis in ("tensor", "dp"):
        stride = 1
        while stride < lax.axis_size(axis):
            steps.append((axis, stride))
            stride *= 2
    order = [down, up, first, second]
    while any(flow.plan for flow in order):
        for flow in order:
            if steps:
                axis, stride = steps.pop(0)
                small = small + swap(small, axis, stride)
            if flow.plan:
                small = flow.advance(small)
    parts = 1 << down.cuts
    grad_down = assemble(down.owner, *down.pieces, parts)
    grad_up = assemble(up.owner, *up.pieces, parts)
    grad_qkv, grad_wout = spread(first.owner, first.pieces, second.pieces, parts)
    return (output, grad_inputs, grad_qkv, grad_wout, grad_up, grad_down, small[:4], small[4:])


def solution(mesh):
    return jax.shard_map(
        per_device,
        mesh=mesh,
        in_specs=(
            P(("dp", "tensor"), None),
            P("dp", None),
            P(None, None, "tensor"),
            P("tensor", None),
            P(None, "tensor"),
            P("tensor", None),
            P(),
            P(),
            P(("dp", "tensor"), None),
        ),
        out_specs=(
            P(("dp", "tensor"), None),
            P(("dp", "tensor"), None),
            P(None, None, "tensor"),
            P("tensor", None),
            P(None, "tensor"),
            P("tensor", None),
            P(),
            P(),
        ),
        check_vma=False,
    )
```
